256 devices in a mesh: tm: 16 (over x, y), line: 16 (over z, core).
Axes of the slice: x: 4, y: 4, z: 8, core: 2. Of those that a mesh axis runs over, the one named last changes fastest.
Arguments:
- station_traces: bfloat16 [512, 65536], P('line', 'tm'), may hold values from -6 to 6
- shot_onset_ticks: int32 [256], P('line'), may hold values from 0 to 65535, as said below
- span_place_index: int32 [256], P('line'), may hold values from 0 to 31, as said below
- spectral_keep_flags: int32 [256, 512], replicated, may hold values 0 or 1
Outputs:
- deblended: bfloat16 [512, 512, 1024], P('tm', 'line')
The draws below stay inside these ranges and needn't reach their ends.
Inputs may be any that keep to these rules, and one draw needn't show every extreme that they name: The block of 4096 samples holding shot_onset_ticks[s] owns shot s; each block owns at most 32 shots and one owns exactly 32. `span_place_index`: shots owned by the same block have distinct slots.
All inputs are finite; a program needn't handle non-finite values.
Results may differ from the reference program's by a relative error of at most 0.0078.
Values may be sent and summed in bfloat16 or wider, within the bound.
A program may use at most 64 MiB of HBM per device.

```python
import math
import jax
import jax.numpy as jnp
from jax import lax

SPAN_TICKS = 1024
FREQ = 512
BATCH_TICKS = 4096
REC_DEV = 32
SLOTS = 32
NSHOT = 256
NREC = 512
SAMPLES = 65536
N_TM = 16
N_LINE = 16


def shot_plan(key):
    base = jax.random.fold_in(key, 11)
    key_busy, key_order, key_offset = jax.random.split(base, 3)
    busiest = jax.random.randint(key_busy, (), 0, N_TM)
    ranks = jax.random.permutation(key_order, NSHOT).astype(jnp.int32)
    others = jnp.maximum(ranks - SLOTS, 0)
    heavy = ranks < SLOTS
    span_holders = jnp.where(heavy, busiest, (busiest + 1 + others % (N_TM - 1)) % N_TM)
    slots = jnp.where(heavy, ranks, others // (N_TM - 1))
    offsets = jax.random.randint(key_offset, (NSHOT,), 0, BATCH_TICKS)
    return ((span_holders * BATCH_TICKS + offsets).astype(jnp.int32), slots.astype(jnp.int32))


def draw_shot_onset_ticks(key, part):
    return shot_plan(key)[0]


def draw_span_place_index(key, part):
    return shot_plan(key)[1]


def touch_ends(entries, rng, least, largest):
    longest = entries.shape.index(max(entries.shape))
    spots = []
    for shift in (0, 1):
        where = [jax.random.randint(jax.random.fold_in(rng, axis), (), 0, length) for axis, length in enumerate(entries.shape)]
        where[longest] = (where[longest] + shift) % entries.shape[longest]
        spots.append(tuple(where))
    return entries.at[spots[0]].set(least).at[spots[1]].set(largest)


def block_levels(rng, shape, cuts, smallest, high):
    gain, own = 1.0, jax.random.fold_in(rng, 6)
    for position, shards_of in cuts:
        heights = jnp.exp(jax.random.uniform(jax.random.fold_in(own, position), (shards_of,), jnp.float32, smallest / len(cuts), high / len(cuts)))
        gain = gain * jnp.repeat(heights, shape[position] // shards_of).reshape([-1 if axis == position else 1 for axis in range(len(shape))])
    return gain


def scatter_about(rng, extent, deviation, most, pieces=(), kind=jnp.bfloat16):
    values = deviation * jax.random.normal(rng, extent, jnp.float32)
    if pieces:
        values = values * block_levels(rng, extent, pieces, -0.22, 0.18)
    return jnp.clip(values, -most, most).astype(kind)


def setup_inputs(seed: int = 0) -> dict:
    keys = jax.random.split(jax.random.key(seed), 5)
    return {
        "station_traces": scatter_about(keys[0], (NREC, SAMPLES), 1.0, 6.0, ((0, 16), (1, 16))),
        "shot_onset_ticks": draw_shot_onset_ticks(jax.random.fold_in(keys[4], 71), 0),
        "span_place_index": draw_span_place_index(jax.random.fold_in(keys[4], 71), 0),
        "spectral_keep_flags": touch_ends((jax.random.randint(keys[3], (NSHOT, FREQ), 0, 4) < 3).astype(jnp.int32), jax.random.fold_in(keys[3], 1), 0, 1),
    }


def make_tables(window, shots):
    times = jnp.arange(window, dtype=jnp.int32)
    freqs = jnp.arange(window // 2, dtype=jnp.int32)
    phase = ((times[:, None] * freqs[None, :]) % window).astype(jnp.float32) * (2.0 * math.pi / window)
    cosine = jnp.cos(phase)
    sine = jnp.sin(phase)
    forward = jnp.concatenate([cosine, -sine], axis=1).astype(jnp.bfloat16)
    halves = jnp.where(freqs == 0, 0.5, 1.0).astype(jnp.float32)[:, None]
    inverse = jnp.concatenate([halves * cosine.T, -halves * sine.T], axis=0).astype(jnp.bfloat16)
    order = jnp.arange(shots, dtype=jnp.int32)
    turn = ((order[:, None] * order[None, :]) % shots).astype(jnp.float32) * (2.0 * math.pi / shots)
    return forward, inverse, jnp.cos(turn).astype(jnp.bfloat16), jnp.sin(turn).astype(jnp.bfloat16)


def filter_gathers(station_panels, keep_mask, tables):
    forward, inverse, shot_cos, shot_sin = tables
    shots, count_here, window = station_panels.shape
    freqs = window // 2
    spectrum = jnp.dot(station_panels.reshape(shots * count_here, window), forward, preferred_element_type=jnp.float32)
    spectrum = spectrum.astype(jnp.bfloat16).reshape(shots, count_here * window)
    cos_part = jnp.dot(shot_cos, spectrum, preferred_element_type=jnp.float32).reshape(shots, count_here, 2, freqs)
    sin_part = jnp.dot(shot_sin, spectrum, preferred_element_type=jnp.float32).reshape(shots, count_here, 2, freqs)
    sign_pair = jnp.array([1.0, -1.0], dtype=jnp.float32)[:, None]
    masked = (cos_part + sin_part[:, :, ::-1, :] * sign_pair) * keep_mask[:, None, None, :]
    masked = masked.astype(jnp.bfloat16).reshape(shots, count_here * window)
    cos_back = jnp.dot(shot_cos, masked, preferred_element_type=jnp.float32).reshape(shots, count_here, 2, freqs)
    sin_back = jnp.dot(shot_sin, masked, preferred_element_type=jnp.float32).reshape(shots, count_here, 2, freqs)
    mixed = (cos_back - sin_back[:, :, ::-1, :] * sign_pair).astype(jnp.bfloat16).reshape(shots * count_here, window)
    filtered = jnp.dot(mixed, inverse, preferred_element_type=jnp.float32) * (2.0 / (window * shots))
    return filtered.astype(jnp.bfloat16).reshape(shots, count_here, window)


def reference(station_traces, shot_onset_ticks, span_place_index, spectral_keep_flags):
    tables = make_tables(SPAN_TICKS, NSHOT)
    keep_mask = spectral_keep_flags.astype(jnp.float32)
    span_holders = shot_onset_ticks // BATCH_TICKS
    slot_code = span_holders * SLOTS + span_place_index
    all_codes = jnp.arange(N_TM * SLOTS, dtype=jnp.int32)
    matched = slot_code[:, None] == all_codes[None, :]
    sources = jnp.arange(NSHOT, dtype=jnp.int32)
    summed = jnp.sum(jnp.where(matched, sources[:, None], 0), axis=0)
    slot_source = jnp.where(jnp.any(matched, axis=0), summed, NSHOT).astype(jnp.int32)
    padded = jnp.pad(station_traces, ((0, 0), (0, SPAN_TICKS)))

    def one_block(block_index, result):
        trace_batch = lax.dynamic_slice_in_dim(padded, block_index * REC_DEV, REC_DEV, 0)
        station_panels = jax.vmap(lambda first_tick_shift: lax.dynamic_slice_in_dim(trace_batch, first_tick_shift, SPAN_TICKS, 1))(shot_onset_ticks)
        filtered = filter_gathers(station_panels, keep_mask, tables)
        slotted = jnp.take(filtered, slot_source, axis=0, mode="fill", fill_value=0)
        return lax.dynamic_update_slice_in_dim(result, slotted, block_index * REC_DEV, 1)

    empty_out = jnp.zeros((N_TM * SLOTS, NREC, SPAN_TICKS), jnp.bfloat16)
    return lax.fori_loop(0, N_LINE, one_block, empty_out)
```

```python
import functools

import jax
import jax.numpy as jnp
import ml_dtypes
import numpy as np
from jax import lax
from jax.experimental import pallas as pl
from jax.experimental.pallas import tpu as pltpu
from jax.sharding import PartitionSpec as P

MESH = pl.DeviceIdType.MESH
LANES = 128
VMEM_LIMIT = 56 << 20
NT = (((1,), (1,)), ((), ()))


def make_tables(window, shots):
    freqs = window // 2
    phase = (np.outer(np.arange(window), np.arange(freqs)) % window) * (2.0 * np.pi / window)
    forward = np.concatenate([np.cos(phase), -np.sin(phase)], axis=1)
    angle = (np.outer(np.arange(shots), np.arange(shots)) % shots) * (2.0 * np.pi / shots)
    turn = np.concatenate([np.cos(angle), np.sin(angle)], axis=1)
    return (
        forward.astype(np.float32).astype(ml_dtypes.bfloat16),
        turn.astype(np.float32).astype(ml_dtypes.bfloat16),
    )


def torus_offsets(side):
    def hops(offset):
        return sum(min(step, side - step) for step in offset)

    every = [(dx, dy) for dx in range(side) for dy in range(side)]
    return sorted(every, key=hops)[1:]


def tm_peer(me, side, offset, sign=1):
    dx, dy = offset
    row = lax.rem(me // side + sign * dx + side, side)
    column = lax.rem(me % side + sign * dy + side, side)
    return row * side + column


def exchange_kernel(
    tm_count, line_count, side,
    blocks_ref, onset_ref, place_ref,
    records_ref, meta_ref,
    mine_ref, heard_ref, own_sem, tm_send, tm_recv, line_send, line_recv,
):
    me, line = lax.axis_index("tm"), lax.axis_index("line")
    offsets = torus_offsets(side)
    rows = blocks_ref.shape[1]
    local_shots = onset_ref.shape[0]
    barrier = pltpu.get_barrier_semaphore()
    for offset in offsets:
        pl.semaphore_signal(
            barrier, inc=1, device_id={"tm": tm_peer(me, side, offset, -1)}, device_id_type=MESH
        )
    for step in range(1, line_count):
        pl.semaphore_signal(
            barrier, inc=1, device_id={"line": lax.rem(line + step, line_count)}, device_id_type=MESH
        )
    shape = mine_ref.shape
    lane = lax.broadcasted_iota(jnp.int32, shape, 1) - line * local_shots
    first_row = lax.broadcasted_iota(jnp.int32, shape, 0) == 0
    mine = jnp.zeros(shape, jnp.int32)
    for i in range(local_shots):
        mine = jnp.where(lane == i, jnp.where(first_row, onset_ref[i], place_ref[i]), mine)
    mine_ref[...] = mine
    heard_ref[0] = mine
    own = pltpu.make_async_copy(
        blocks_ref.at[me], records_ref.at[pl.ds(pl.multiple_of(me * rows, rows), rows)], own_sem
    )
    own.start()
    pl.semaphore_wait(barrier, len(offsets) + line_count - 1)
    copies = []
    for step in range(1, line_count):
        copies.append(
            pltpu.make_async_remote_copy(
                mine_ref, heard_ref.at[step], line_send.at[step], line_recv.at[step],
                device_id={"line": lax.rem(line + step, line_count)}, device_id_type=MESH,
            )
        )
        copies[-1].start()
    for i, offset in enumerate(offsets):
        peer = tm_peer(me, side, offset)
        copies.append(
            pltpu.make_async_remote_copy(
                blocks_ref.at[peer],
                records_ref.at[pl.ds(pl.multiple_of(me * rows, rows), rows)],
                tm_send.at[i], tm_recv.at[i],
                device_id={"tm": peer}, device_id_type=MESH,
            )
        )
        copies[-1].start()
    own.wait()
    for copy in copies[: line_count - 1]:
        copy.wait()
    total = heard_ref[0]
    for step in range(1, line_count):
        total = total + heard_ref[step]
    meta_ref[...] = total
    for copy in copies[line_count - 1 :]:
        copy.wait()


def exchange(blocks, onsets, places, tm_count, line_count):
    side = int(round(tm_count**0.5))
    shots = onsets.shape[0] * line_count
    dma = pltpu.SemaphoreType.DMA
    return pl.pallas_call(
        functools.partial(exchange_kernel, tm_count, line_count, side),
        out_shape=(
            jax.ShapeDtypeStruct((tm_count * blocks.shape[1], LANES), jnp.bfloat16),
            jax.ShapeDtypeStruct((8, shots), jnp.int32),
        ),
        in_specs=[
            pl.BlockSpec(memory_space=pltpu.VMEM),
            pl.BlockSpec(memory_space=pltpu.SMEM),
            pl.BlockSpec(memory_space=pltpu.SMEM),
        ],
        out_specs=(
            pl.BlockSpec(memory_space=pltpu.VMEM),
            pl.BlockSpec(memory_space=pltpu.VMEM),
        ),
        scratch_shapes=[
            pltpu.VMEM((8, shots), jnp.int32),
            pltpu.VMEM((line_count, 8, shots), jnp.int32),
            dma, dma((tm_count,)), dma((tm_count,)), dma((line_count,)), dma((line_count,)),
        ],
        compiler_params=pltpu.CompilerParams(
            collective_id=0, has_side_effects=True, vmem_limit_bytes=8 << 20
        ),
        name="exchange_records",
    )(blocks, onsets, places)


def filter_kernel(
    block_len, capacity,
    onset_ref, meta_ref, records_ref, keep_ref, forward_hbm, turn_ref,
    mixed_ref,
    wide_ref, cut_ref, panels_ref, spectrum_ref, chosen_ref, forward_ref, sem,
):
    shots, freqs = keep_ref.shape
    window = 2 * freqs
    chunks = window // LANES
    pair = 2
    per_shot = pair * chunks
    record_rows = records_ref.shape[0]
    load = pltpu.make_async_copy(forward_hbm, forward_ref, sem)
    load.start()
    wide_ref[:record_rows] = records_ref[...].astype(jnp.float32)
    wide_ref[record_rows:] = jnp.zeros(
        (wide_ref.shape[0] - record_rows, LANES), jnp.float32
    )
    lane = lax.broadcasted_iota(jnp.int32, (per_shot, LANES), 1)

    def cut(shot):
        start = onset_ref[0, shot]
        base = (start // LANES) * pair
        within = lax.rem(start, LANES)
        here = wide_ref[pl.ds(base, per_shot), :]
        following = wide_ref[pl.ds(base + pair, per_shot), :]
        both = jnp.where(lane >= within, here, following)
        turned = pltpu.roll(both, lax.rem(LANES - within, LANES), 1)
        cut_ref[pl.ds(pl.multiple_of(shot * per_shot, per_shot), per_shot), :] = turned

    group = 8

    @pl.loop(0, shots // group)
    def _(step):
        for i in range(group):
            cut(step * group + i)

    for rec in range(pair):
        for chunk in range(chunks):
            panels_ref[rec * shots : (rec + 1) * shots, chunk * LANES : (chunk + 1) * LANES] = (
                cut_ref[pl.ds(pair * chunk + rec, shots, stride=per_shot), :].astype(jnp.bfloat16)
            )
    load.wait()
    width = 256

    @pl.loop(0, window // width)
    def _(step):
        columns = pl.ds(pl.multiple_of(step * width, width), width)
        spectrum_ref[:, columns] = jnp.dot(
            panels_ref[...], forward_ref[:, columns], preferred_element_type=jnp.float32
        ).astype(jnp.bfloat16)

    code = (meta_ref[0:1, :] // block_len) * capacity + meta_ref[1:2, :]
    slots = chosen_ref.shape[0]
    picked = (lax.broadcasted_iota(jnp.int32, (slots, shots), 0) == code).astype(jnp.float32)
    chosen_ref[...] = jnp.dot(
        picked.astype(jnp.bfloat16), turn_ref[...], preferred_element_type=jnp.float32
    ).astype(jnp.bfloat16)
    owners = slots // capacity
    half = jnp.float32(0.5)

    @pl.loop(0, pair * (freqs // width))
    def _(step):
        rec = step // (freqs // width)
        part = lax.rem(step, freqs // width)
        low = pl.ds(pl.multiple_of(part * width, width), width)
        high = pl.ds(pl.multiple_of(freqs + part * width, width), width)
        rows = pl.ds(pl.multiple_of(rec * shots, shots), shots)
        a, b = spectrum_ref[rows, low], spectrum_ref[rows, high]
        keep = keep_ref[:, low].astype(jnp.float32)
        turn = turn_ref[...]
        p = jnp.dot(turn, jnp.concatenate([a, b], axis=0), preferred_element_type=jnp.float32)
        q = jnp.dot(turn, jnp.concatenate([b, -a], axis=0), preferred_element_type=jnp.float32)
        p, q = (p * keep).astype(jnp.bfloat16), (q * keep).astype(jnp.bfloat16)
        chosen = chosen_ref[...]
        ma = jnp.dot(chosen, jnp.concatenate([p, -q], axis=0), preferred_element_type=jnp.float32)
        mb = jnp.dot(chosen, jnp.concatenate([q, p], axis=0), preferred_element_type=jnp.float32)
        first = lax.broadcasted_iota(jnp.int32, (slots, width), 1) + part * width == 0
        ma = jnp.where(first, ma * half, ma).astype(jnp.bfloat16)
        mb = jnp.where(first, mb * half, mb).astype(jnp.bfloat16)
        for owner in range(owners):
            mine = slice(owner * capacity, (owner + 1) * capacity)
            there = pl.ds(pl.multiple_of(rec * capacity, capacity), capacity)
            mixed_ref[owner, there, low] = ma[mine]
            mixed_ref[owner, there, high] = mb[mine]


def filter_records(meta, records, keep_flags, forward, turn, tm_count, block_len):
    shots, freqs = keep_flags.shape
    window = 2 * freqs
    capacity = 2 * shots // tm_count
    vmem = pl.BlockSpec(memory_space=pltpu.VMEM)
    return pl.pallas_call(
        functools.partial(filter_kernel, block_len, capacity),
        out_shape=jax.ShapeDtypeStruct((tm_count, 2 * capacity, window), jnp.bfloat16),
        in_specs=[
            pl.BlockSpec(memory_space=pltpu.SMEM), vmem, vmem, vmem,
            pl.BlockSpec(memory_space=pl.ANY), vmem,
        ],
        out_specs=vmem,
        scratch_shapes=[
            pltpu.VMEM((records.shape[0] + 4 * window // LANES, LANES), jnp.float32),
            pltpu.VMEM((2 * shots * window // LANES, LANES), jnp.float32),
            pltpu.VMEM((2 * shots, window), jnp.bfloat16),
            pltpu.VMEM((2 * shots, window), jnp.bfloat16),
            pltpu.VMEM((tm_count * capacity, 2 * shots), jnp.bfloat16),
            pltpu.VMEM((window, window), jnp.bfloat16),
            pltpu.SemaphoreType.DMA,
        ],
        compiler_params=pltpu.CompilerParams(vmem_limit_bytes=VMEM_LIMIT),
        name="filter_records",
    )(meta, meta, records, keep_flags, forward, turn)


def deliver_kernel(
    tm_count, side, batch,
    mixed_ref, forward_hbm,
    traces_ref,
    arrived_ref, forward_ref, load_sem, own_sem, send_sem, recv_sem,
):
    me = lax.axis_index("tm")
    offsets = [(0, 0)] + torus_offsets(side)
    rows = mixed_ref.shape[1]
    capacity = rows // 2
    window = mixed_ref.shape[2]
    load = pltpu.make_async_copy(forward_hbm, forward_ref, load_sem)
    load.start()
    barrier = pltpu.get_barrier_semaphore()
    for offset in offsets[1:]:
        pl.semaphore_signal(
            barrier, inc=1, device_id={"tm": tm_peer(me, side, offset, -1)}, device_id_type=MESH
        )
    own = pltpu.make_async_copy(mixed_ref.at[me], arrived_ref.at[0], own_sem)
    own.start()
    pl.semaphore_wait(barrier, tm_count - 1)
    copies = [own]
    for i, offset in enumerate(offsets):
        if i == 0:
            continue
        peer = tm_peer(me, side, offset)
        copies.append(
            pltpu.make_async_remote_copy(
                mixed_ref.at[peer], arrived_ref.at[i], send_sem.at[i], recv_sem.at[i],
                device_id={"tm": peer}, device_id_type=MESH,
            )
        )
        copies[-1].start()
    load.wait()
    width = 256
    scale = jnp.float32(4.0 / (window * tm_count * capacity))
    for first in range(0, tm_count, batch):
        for i in range(first, first + batch):
            if i == 0:
                own.wait()
            else:
                copies[i].wait_recv()
        sources = [tm_peer(me, side, offsets[i], -1) for i in range(first, first + batch)]

        @pl.loop(0, window // width)
        def _(step):
            columns = pl.ds(pl.multiple_of(step * width, width), width)
            block = arrived_ref[first : first + batch].reshape(batch * rows, window)
            out = lax.dot_general(
                block, forward_ref[columns, :], NT, preferred_element_type=jnp.float32
            ) * scale
            for i in range(batch):
                for rec in range(2):
                    at = i * rows + rec * capacity
                    for tile in range(width // LANES):
                        traces_ref[
                            step * (width // LANES) + tile,
                            pl.ds(sources[i] * 2 + rec, capacity, stride=2 * tm_count),
                            :,
                        ] = out[at : at + capacity, tile * LANES : (tile + 1) * LANES]

    for copy in copies[1:]:
        copy.wait_send()


def deliver(mixed, forward, batch=4):
    tm_count, rows, window = mixed.shape
    side = int(round(tm_count**0.5))
    dma = pltpu.SemaphoreType.DMA
    return pl.pallas_call(
        functools.partial(deliver_kernel, tm_count, side, batch),
        out_shape=jax.ShapeDtypeStruct((window // LANES, tm_count * rows, LANES), jnp.float32),
        in_specs=[
            pl.BlockSpec(memory_space=pltpu.VMEM),
            pl.BlockSpec(memory_space=pl.ANY),
        ],
        out_specs=pl.BlockSpec(memory_space=pltpu.VMEM),
        scratch_shapes=[
            pltpu.VMEM(mixed.shape, jnp.bfloat16),
            pltpu.VMEM(forward.shape, jnp.bfloat16),
            dma, dma, dma((tm_count,)), dma((tm_count,)),
        ],
        compiler_params=pltpu.CompilerParams(
            collective_id=1, has_side_effects=True, vmem_limit_bytes=VMEM_LIMIT
        ),
        name="deliver_windows",
    )(mixed, forward)


def on_device(station_traces, shot_onset_ticks, span_place_index, spectral_keep_flags):
    tm_count, line_count = lax.axis_size("tm"), lax.axis_size("line")
    rec_rows, block_len = station_traces.shape
    shots, freqs = spectral_keep_flags.shape
    window = 2 * freqs
    forward, turn = make_tables(window, shots)
    forward, turn = jnp.asarray(forward), jnp.asarray(turn)
    blocks = station_traces.reshape(tm_count, rec_rows // tm_count, block_len // LANES, LANES)
    blocks = jnp.swapaxes(blocks, 1, 2).reshape(tm_count, -1, LANES)
    records, meta = exchange(blocks, shot_onset_ticks, span_place_index, tm_count, line_count)
    mixed = filter_records(
        meta, records, spectral_keep_flags, forward, turn, tm_count, block_len
    )
    traces = deliver(mixed, forward)
    traces = jnp.swapaxes(traces.astype(jnp.bfloat16), 0, 1)
    return traces.reshape(2 * shots // tm_count, rec_rows, window)


def solution(mesh):
    in_specs = (P("line", "tm"), P("line"), P("line"), P())
    out_specs = P("tm", "line", None)
    return jax.shard_map(
        on_device, mesh=mesh, in_specs=in_specs, out_specs=out_specs, check_vma=False
    )
```

```python
import functools

import jax
import jax.numpy as jnp
import ml_dtypes
import numpy as np
from jax import lax
from jax.experimental import pallas as pl
from jax.experimental.pallas import tpu as pltpu
from jax.sharding import PartitionSpec as P

MESH = pl.DeviceIdType.MESH
LANES = 128
NT = (((1,), (1,)), ((), ()))


def make_tables(window, shots):
    freqs = window // 2
    phase = (np.outer(np.arange(window), np.arange(freqs)) % window) * (2.0 * np.pi / window)
    forward = np.concatenate([np.cos(phase), -np.sin(phase)], axis=1)
    angle = (np.outer(np.arange(shots), np.arange(shots)) % shots) * (2.0 * np.pi / shots)
    turn = np.concatenate([np.cos(angle), np.sin(angle)], axis=1)
    return (
        forward.astype(np.float32).astype(ml_dtypes.bfloat16),
        turn.astype(np.float32).astype(ml_dtypes.bfloat16),
    )


def torus_offsets(side):
    def hops(offset):
        return sum(min(step, side - step) for step in offset)

    every = [(dx, dy) for dx in range(side) for dy in range(side)]
    return sorted(every, key=hops)[1:]


def tm_peer(me, side, offset, sign=1):
    dx, dy = offset
    row = lax.rem(me // side + sign * dx + side, side)
    column = lax.rem(me % side + sign * dy + side, side)
    return row * side + column


def exchange_kernel(
    tm_count, line_count, side,
    blocks_ref, onset_ref, place_ref,
    records_ref, meta_ref,
    mine_ref, heard_ref, own_sem, tm_send, tm_recv, line_send, line_recv,
):
    me, line = lax.axis_index("tm"), lax.axis_index("line")
    offsets = torus_offsets(side)
    rows = blocks_ref.shape[1]
    local_shots = onset_ref.shape[0]
    barrier = pltpu.get_barrier_semaphore()
    for offset in offsets:
        pl.semaphore_signal(
            barrier, inc=1, device_id={"tm": tm_peer(me, side, offset, -1)}, device_id_type=MESH
        )
    for step in range(1, line_count):
        pl.semaphore_signal(
            barrier, inc=1, device_id={"line": lax.rem(line + step, line_count)}, device_id_type=MESH
        )
    shape = mine_ref.shape
    lane = lax.broadcasted_iota(jnp.int32, shape, 1) - line * local_shots
    first_row = lax.broadcasted_iota(jnp.int32, shape, 0) == 0
    mine = jnp.zeros(shape, jnp.int32)
    for i in range(local_shots):
        mine = jnp.where(lane == i, jnp.where(first_row, onset_ref[i], place_ref[i]), mine)
    mine_ref[...] = mine
    heard_ref[0] = mine
    own = pltpu.make_async_copy(
        blocks_ref.at[me], records_ref.at[pl.ds(pl.multiple_of(me * rows, rows), rows)], own_sem
    )
    own.start()
    pl.semaphore_wait(barrier, len(offsets) + line_count - 1)
    copies = []
    for step in range(1, line_count):
        copies.append(
            pltpu.make_async_remote_copy(
                mine_ref, heard_ref.at[step], line_send.at[step], line_recv.at[step],
                device_id={"line": lax.rem(line + step, line_count)}, device_id_type=MESH,
            )
        )
        copies[-1].start()
    for i, offset in enumerate(offsets):
        peer = tm_peer(me, side, offset)
        copies.append(
            pltpu.make_async_remote_copy(
                blocks_ref.at[peer],
                records_ref.at[pl.ds(pl.multiple_of(me * rows, rows), rows)],
                tm_send.at[i], tm_recv.at[i],
                device_id={"tm": peer}, device_id_type=MESH,
            )
        )
        copies[-1].start()
    own.wait()
    for copy in copies[: line_count - 1]:
        copy.wait()
    total = heard_ref[0]
    for step in range(1, line_count):
        total = total + heard_ref[step]
    meta_ref[...] = total
    for copy in copies[line_count - 1 :]:
        copy.wait()


def exchange(blocks, onsets, places, tm_count, line_count):
    side = int(round(tm_count**0.5))
    shots = onsets.shape[0] * line_count
    dma = pltpu.SemaphoreType.DMA
    return pl.pallas_call(
        functools.partial(exchange_kernel, tm_count, line_count, side),
        out_shape=(
            jax.ShapeDtypeStruct((tm_count * blocks.shape[1], LANES), jnp.bfloat16),
            jax.ShapeDtypeStruct((8, shots), jnp.int32),
        ),
        in_specs=[
            pl.BlockSpec(memory_space=pltpu.VMEM),
            pl.BlockSpec(memory_space=pltpu.SMEM),
            pl.BlockSpec(memory_space=pltpu.SMEM),
        ],
        out_specs=(
            pl.BlockSpec(memory_space=pltpu.VMEM),
            pl.BlockSpec(memory_space=pltpu.VMEM),
        ),
        scratch_shapes=[
            pltpu.VMEM((8, shots), jnp.int32),
            pltpu.VMEM((line_count, 8, shots), jnp.int32),
            dma, dma((tm_count,)), dma((tm_count,)), dma((line_count,)), dma((line_count,)),
        ],
        compiler_params=pltpu.CompilerParams(
            collective_id=0, has_side_effects=True, vmem_limit_bytes=8 << 20
        ),
        name="exchange_records",
    )(blocks, onsets, places)


def filter_kernel(
    block_len, capacity,
    onset_ref, meta_ref, records_ref, keep_ref, forward_hbm, turn_ref,
    mixed_ref,
    wide_ref, cut_ref, panels_ref, spectrum_ref, chosen_ref, forward_ref, sem,
):
    shots, freqs = keep_ref.shape
    window = 2 * freqs
    chunks = window // LANES
    pair = 2
    per_shot = pair * chunks
    record_rows = records_ref.shape[0]
    load = pltpu.make_async_copy(forward_hbm, forward_ref, sem)
    load.start()
    wide_ref[:record_rows] = records_ref[...].astype(jnp.float32)
    wide_ref[record_rows:] = jnp.zeros(
        (wide_ref.shape[0] - record_rows, LANES), jnp.float32
    )
    lane = lax.broadcasted_iota(jnp.int32, (per_shot, LANES), 1)

    def cut(shot):
        start = onset_ref[0, shot]
        base = (start // LANES) * pair
        within = lax.rem(start, LANES)
        here = wide_ref[pl.ds(base, per_shot), :]
        following = wide_ref[pl.ds(base + pair, per_shot), :]
        both = jnp.where(lane >= within, here, following)
        turned = pltpu.roll(both, lax.rem(LANES - within, LANES), 1)
        cut_ref[pl.ds(pl.multiple_of(shot * per_shot, per_shot), per_shot), :] = turned

    group = 8

    @pl.loop(0, shots // group)
    def _(step):
        for i in range(group):
            cut(step * group + i)

    for rec in range(pair):
        for chunk in range(chunks):
            panels_ref[rec * shots : (rec + 1) * shots, chunk * LANES : (chunk + 1) * LANES] = (
                cut_ref[pl.ds(pair * chunk + rec, shots, stride=per_shot), :].astype(jnp.bfloat16)
            )
    load.wait()
    width = 256

    @pl.loop(0, window // width)
    def _(step):
        columns = pl.ds(pl.multiple_of(step * width, width), width)
        spectrum_ref[:, columns] = jnp.dot(
            panels_ref[...], forward_ref[:, columns], preferred_element_type=jnp.float32
        ).astype(jnp.bfloat16)

    code = (meta_ref[0:1, :] // block_len) * capacity + meta_ref[1:2, :]
    slots = chosen_ref.shape[0]
    picked = (lax.broadcasted_iota(jnp.int32, (slots, shots), 0) == code).astype(jnp.float32)
    chosen_ref[...] = jnp.dot(
        picked.astype(jnp.bfloat16), turn_ref[...], preferred_element_type=jnp.float32
    ).astype(jnp.bfloat16)
    owners = slots // capacity
    half = jnp.float32(0.5)

    @pl.loop(0, pair * (freqs // width))
    def _(step):
        rec = step // (freqs // width)
        part = lax.rem(step, freqs // width)
        low = pl.ds(pl.multiple_of(part * width, width), width)
        high = pl.ds(pl.multiple_of(freqs + part * width, width), width)
        rows = pl.ds(pl.multiple_of(rec * shots, shots), shots)
        a, b = spectrum_ref[rows, low], spectrum_ref[rows, high]
        keep = keep_ref[:, low].astype(jnp.float32)
        turn = turn_ref[...]
        p = jnp.dot(turn, jnp.concatenate([a, b], axis=0), preferred_element_type=jnp.float32)
        q = jnp.dot(turn, jnp.concatenate([b, -a], axis=0), preferred_element_type=jnp.float32)
        p, q = (p * keep).astype(jnp.bfloat16), (q * keep).astype(jnp.bfloat16)
        chosen = chosen_ref[...]
        ma = jnp.dot(chosen, jnp.concatenate([p, -q], axis=0), preferred_element_type=jnp.float32)
        mb = jnp.dot(chosen, jnp.concatenate([q, p], axis=0), preferred_element_type=jnp.float32)
        first = lax.broadcasted_iota(jnp.int32, (slots, width), 1) + part * width == 0
        ma = jnp.where(first, ma * half, ma).astype(jnp.bfloat16)
        mb = jnp.where(first, mb * half, mb).astype(jnp.bfloat16)
        for owner in range(owners):
            mine = slice(owner * capacity, (owner + 1) * capacity)
            there = pl.ds(pl.multiple_of(rec * capacity, capacity), capacity)
            mixed_ref[owner, there, low] = ma[mine]
            mixed_ref[owner, there, high] = mb[mine]


def filter_records(meta, records, keep_flags, forward, turn, tm_count, block_len):
    shots, freqs = keep_flags.shape
    window = 2 * freqs
    capacity = 2 * shots // tm_count
    vmem = pl.BlockSpec(memory_space=pltpu.VMEM)
    return pl.pallas_call(
        functools.partial(filter_kernel, block_len, capacity),
        out_shape=jax.ShapeDtypeStruct((tm_count, 2 * capacity, window), jnp.bfloat16),
        in_specs=[
            pl.BlockSpec(memory_space=pltpu.SMEM), vmem, vmem, vmem,
            pl.BlockSpec(memory_space=pl.ANY), vmem,
        ],
        out_specs=vmem,
        scratch_shapes=[
            pltpu.VMEM((records.shape[0] + 4 * window // LANES, LANES), jnp.float32),
            pltpu.VMEM((2 * shots * window // LANES, LANES), jnp.float32),
            pltpu.VMEM((2 * shots, window), jnp.bfloat16),
            pltpu.VMEM((2 * shots, window), jnp.bfloat16),
            pltpu.VMEM((tm_count * capacity, 2 * shots), jnp.bfloat16),
            pltpu.VMEM((window, window), jnp.bfloat16),
            pltpu.SemaphoreType.DMA,
        ],
        compiler_params=pltpu.CompilerParams(vmem_limit_bytes=24 << 20),
        name="filter_records",
    )(meta, meta, records, keep_flags, forward, turn)


def deliver_kernel(
    tm_count, side, batch,
    mixed_ref, forward_hbm,
    traces_ref,
    arrived_ref, forward_ref, load_sem, own_sem, send_sem, recv_sem,
):
    me = lax.axis_index("tm")
    offsets = [(0, 0)] + torus_offsets(side)
    rows = mixed_ref.shape[1]
    capacity = rows // 2
    window = mixed_ref.shape[2]
    load = pltpu.make_async_copy(forward_hbm, forward_ref, load_sem)
    load.start()
    barrier = pltpu.get_barrier_semaphore()
    for offset in offsets[1:]:
        pl.semaphore_signal(
            barrier, inc=1, device_id={"tm": tm_peer(me, side, offset, -1)}, device_id_type=MESH
        )
    own = pltpu.make_async_copy(mixed_ref.at[me], arrived_ref.at[0], own_sem)
    own.start()
    pl.semaphore_wait(barrier, tm_count - 1)
    copies = [own]
    for i, offset in enumerate(offsets):
        if i == 0:
            continue
        peer = tm_peer(me, side, offset)
        copies.append(
            pltpu.make_async_remote_copy(
                mixed_ref.at[peer], arrived_ref.at[i], send_sem.at[i], recv_sem.at[i],
                device_id={"tm": peer}, device_id_type=MESH,
            )
        )
        copies[-1].start()
    load.wait()
    width = 256
    scale = jnp.float32(4.0 / (window * tm_count * capacity))
    for first in range(0, tm_count, batch):
        for i in range(first, first + batch):
            if i == 0:
                own.wait()
            else:
                copies[i].wait_recv()
        sources = [tm_peer(me, side, offsets[i], -1) for i in range(first, first + batch)]

        @pl.loop(0, window // width)
        def _(step):
            columns = pl.ds(pl.multiple_of(step * width, width), width)
            block = arrived_ref[first : first + batch].reshape(batch * rows, window)
            out = lax.dot_general(
                block, forward_ref[columns, :], NT, preferred_element_type=jnp.float32
            ) * scale
            for i in range(batch):
                for rec in range(2):
                    at = i * rows + rec * capacity
                    for tile in range(width // LANES):
                        traces_ref[
                            step * (width // LANES) + tile,
                            pl.ds(sources[i] * 2 + rec, capacity, stride=2 * tm_count),
                            :,
                        ] = out[at : at + capacity, tile * LANES : (tile + 1) * LANES]

    for copy in copies[1:]:
        copy.wait_send()


def deliver(mixed, forward, batch=4):
    tm_count, rows, window = mixed.shape
    side = int(round(tm_count**0.5))
    dma = pltpu.SemaphoreType.DMA
    return pl.pallas_call(
        functools.partial(deliver_kernel, tm_count, side, batch),
        out_shape=jax.ShapeDtypeStruct((window // LANES, tm_count * rows, LANES), jnp.float32),
        in_specs=[
            pl.BlockSpec(memory_space=pltpu.VMEM),
            pl.BlockSpec(memory_space=pl.ANY),
        ],
        out_specs=pl.BlockSpec(memory_space=pltpu.VMEM),
        scratch_shapes=[
            pltpu.VMEM(mixed.shape, jnp.bfloat16),
            pltpu.VMEM(forward.shape, jnp.bfloat16),
            dma, dma, dma((tm_count,)), dma((tm_count,)),
        ],
        compiler_params=pltpu.CompilerParams(
            collective_id=1, has_side_effects=True, vmem_limit_bytes=24 << 20
        ),
        name="deliver_windows",
    )(mixed, forward)


def place_kernel(traces_ref, placed_ref, staged_ref, sem):
    slots, receivers, _ = staged_ref.shape

    def out_copy(slot):
        return pltpu.make_async_copy(staged_ref.at[slot], placed_ref.at[slot], sem.at[slot])

    @pl.loop(0, slots)
    def _(slot):
        for tile in range(traces_ref.shape[0]):
            rows = traces_ref[tile, pl.ds(pl.multiple_of(slot * receivers, receivers), receivers), :]
            staged_ref[slot, :, tile * LANES : (tile + 1) * LANES] = rows.astype(jnp.bfloat16)
        out_copy(slot).start()

    @pl.loop(0, slots)
    def _(slot):
        out_copy(slot).wait()


def place(traces, slots, receivers):
    window = traces.shape[0] * LANES
    return pl.pallas_call(
        place_kernel,
        out_shape=jax.ShapeDtypeStruct((slots, receivers, window), jnp.bfloat16),
        in_specs=[pl.BlockSpec(memory_space=pltpu.VMEM)],
        out_specs=pl.BlockSpec(memory_space=pl.ANY),
        scratch_shapes=[
            pltpu.VMEM((slots, receivers, window), jnp.bfloat16),
            pltpu.SemaphoreType.DMA((slots,)),
        ],
        compiler_params=pltpu.CompilerParams(vmem_limit_bytes=12 << 20),
        name="place_windows",
    )(traces)


def on_device(station_traces, shot_onset_ticks, span_place_index, spectral_keep_flags):
    tm_count, line_count = lax.axis_size("tm"), lax.axis_size("line")
    rec_rows, block_len = station_traces.shape
    shots, freqs = spectral_keep_flags.shape
    window = 2 * freqs
    forward, turn = make_tables(window, shots)
    forward, turn = jnp.asarray(forward), jnp.asarray(turn)
    blocks = station_traces.reshape(tm_count, rec_rows // tm_count, block_len // LANES, LANES)
    blocks = jnp.swapaxes(blocks, 1, 2).reshape(tm_count, -1, LANES)
    records, meta = exchange(blocks, shot_onset_ticks, span_place_index, tm_count, line_count)
    mixed = filter_records(
        meta, records, spectral_keep_flags, forward, turn, tm_count, block_len
    )
    traces = deliver(mixed, forward)
    return place(traces, 2 * shots // tm_count, rec_rows)


def solution(mesh):
    in_specs = (P("line", "tm"), P("line"), P("line"), P())
    out_specs = P("tm", "line", None)
    return jax.shard_map(
        on_device, mesh=mesh, in_specs=in_specs, out_specs=out_specs, check_vma=False
    )
```

```python
import functools

import jax
import jax.numpy as jnp
import ml_dtypes
import numpy as np
from jax import lax
from jax.experimental import pallas as pl
from jax.experimental.pallas import tpu as pltpu
from jax.sharding import PartitionSpec as P

MESH = pl.DeviceIdType.MESH
LANES = 128
NT = (((1,), (1,)), ((), ()))


def make_tables(window, shots):
    freqs = window // 2
    phase = (np.outer(np.arange(window), np.arange(freqs)) % window) * (2.0 * np.pi / window)
    forward = np.concatenate([np.cos(phase), -np.sin(phase)], axis=1)
    angle = (np.outer(np.arange(shots), np.arange(shots)) % shots) * (2.0 * np.pi / shots)
    turn = np.concatenate([np.cos(angle), np.sin(angle)], axis=1)
    return (
        forward.astype(np.float32).astype(ml_dtypes.bfloat16),
        turn.astype(np.float32).astype(ml_dtypes.bfloat16),
    )


def torus_offsets(side):
    def hops(offset):
        return sum(min(step, side - step) for step in offset)

    every = [(dx, dy) for dx in range(side) for dy in range(side)]
    return sorted(every, key=hops)[1:]


def tm_peer(me, side, offset, sign=1):
    dx, dy = offset
    row = lax.rem(me // side + sign * dx + side, side)
    column = lax.rem(me % side + sign * dy + side, side)
    return row * side + column


def exchange_kernel(
    tm_count, line_count, side,
    blocks_ref, onset_ref, place_ref, forward_hbm, turn_hbm, keep_hbm,
    records_ref, meta_ref, forward_ref, turn_ref, keep_ref,
    mine_ref, heard_ref, own_sem, load_sem, tm_send, tm_recv, line_send, line_recv,
):
    me, line = lax.axis_index("tm"), lax.axis_index("line")
    offsets = torus_offsets(side)
    rows = blocks_ref.shape[1]
    local_shots = onset_ref.shape[0]
    barrier = pltpu.get_barrier_semaphore()
    for offset in offsets:
        pl.semaphore_signal(
            barrier, inc=1, device_id={"tm": tm_peer(me, side, offset, -1)}, device_id_type=MESH
        )
    for step in range(1, line_count):
        pl.semaphore_signal(
            barrier, inc=1, device_id={"line": lax.rem(line + step, line_count)}, device_id_type=MESH
        )
    loads = [
        pltpu.make_async_copy(there, here, load_sem.at[i])
        for i, (there, here) in enumerate(
            ((forward_hbm, forward_ref), (turn_hbm, turn_ref), (keep_hbm, keep_ref))
        )
    ]
    for load in loads:
        load.start()
    shape = mine_ref.shape
    lane = lax.broadcasted_iota(jnp.int32, shape, 1) - line * local_shots
    first_row = lax.broadcasted_iota(jnp.int32, shape, 0) == 0
    mine = jnp.zeros(shape, jnp.int32)
    for i in range(local_shots):
        mine = jnp.where(lane == i, jnp.where(first_row, onset_ref[i], place_ref[i]), mine)
    mine_ref[...] = mine
    heard_ref[0] = mine
    own = pltpu.make_async_copy(
        blocks_ref.at[me], records_ref.at[pl.ds(pl.multiple_of(me * rows, rows), rows)], own_sem
    )
    own.start()
    pl.semaphore_wait(barrier, len(offsets) + line_count - 1)
    copies = []
    for step in range(1, line_count):
        copies.append(
            pltpu.make_async_remote_copy(
                mine_ref, heard_ref.at[step], line_send.at[step], line_recv.at[step],
                device_id={"line": lax.rem(line + step, line_count)}, device_id_type=MESH,
            )
        )
        copies[-1].start()
    for i, offset in enumerate(offsets):
        peer = tm_peer(me, side, offset)
        copies.append(
            pltpu.make_async_remote_copy(
                blocks_ref.at[peer],
                records_ref.at[pl.ds(pl.multiple_of(me * rows, rows), rows)],
                tm_send.at[i], tm_recv.at[i],
                device_id={"tm": peer}, device_id_type=MESH,
            )
        )
        copies[-1].start()
    own.wait()
    for copy in copies[: line_count - 1]:
        copy.wait()
    total = heard_ref[0]
    for step in range(1, line_count):
        total = total + heard_ref[step]
    meta_ref[...] = total
    for copy in copies[line_count - 1 :]:
        copy.wait()
    for load in loads:
        load.wait()


def exchange(blocks, onsets, places, tables, tm_count, line_count):
    side = int(round(tm_count**0.5))
    shots = onsets.shape[0] * line_count
    dma = pltpu.SemaphoreType.DMA
    return pl.pallas_call(
        functools.partial(exchange_kernel, tm_count, line_count, side),
        out_shape=(
            jax.ShapeDtypeStruct((tm_count * blocks.shape[1], LANES), jnp.bfloat16),
            jax.ShapeDtypeStruct((8, shots), jnp.int32),
            *(jax.ShapeDtypeStruct(table.shape, table.dtype) for table in tables),
        ),
        in_specs=[
            pl.BlockSpec(memory_space=pltpu.VMEM),
            pl.BlockSpec(memory_space=pltpu.SMEM),
            pl.BlockSpec(memory_space=pltpu.SMEM),
            *(pl.BlockSpec(memory_space=pl.ANY) for _ in tables),
        ],
        out_specs=tuple(pl.BlockSpec(memory_space=pltpu.VMEM) for _ in range(2 + len(tables))),
        scratch_shapes=[
            pltpu.VMEM((8, shots), jnp.int32),
            pltpu.VMEM((line_count, 8, shots), jnp.int32),
            dma, dma((len(tables),)), dma((tm_count,)), dma((tm_count,)), dma((line_count,)), dma((line_count,)),
        ],
        compiler_params=pltpu.CompilerParams(
            collective_id=0, has_side_effects=True, vmem_limit_bytes=49 << 20
        ),
        name="exchange_records",
    )(blocks, onsets, places, *tables)


def filter_kernel(
    block_len, capacity,
    onset_ref, meta_ref, records_ref, keep_ref, forward_ref, turn_ref,
    mixed_ref,
    wide_ref, cut_ref, panels_ref, spectrum_ref, chosen_ref,
):
    shots, freqs = keep_ref.shape
    window = 2 * freqs
    chunks = window // LANES
    pair = 2
    per_shot = pair * chunks
    record_rows = records_ref.shape[0]
    wide_ref[:record_rows] = records_ref[...].astype(jnp.float32)
    wide_ref[record_rows:] = jnp.zeros(
        (wide_ref.shape[0] - record_rows, LANES), jnp.float32
    )
    lane = lax.broadcasted_iota(jnp.int32, (per_shot, LANES), 1)

    def cut(shot):
        start = onset_ref[0, shot]
        base = (start // LANES) * pair
        within = lax.rem(start, LANES)
        here = wide_ref[pl.ds(base, per_shot), :]
        following = wide_ref[pl.ds(base + pair, per_shot), :]
        both = jnp.where(lane >= within, here, following)
        turned = pltpu.roll(both, lax.rem(LANES - within, LANES), 1)
        cut_ref[pl.ds(pl.multiple_of(shot * per_shot, per_shot), per_shot), :] = turned

    group = 8

    @pl.loop(0, shots // group)
    def _(step):
        for i in range(group):
            cut(step * group + i)

    for rec in range(pair):
        for chunk in range(chunks):
            panels_ref[rec * shots : (rec + 1) * shots, chunk * LANES : (chunk + 1) * LANES] = (
                cut_ref[pl.ds(pair * chunk + rec, shots, stride=per_shot), :].astype(jnp.bfloat16)
            )
    width = 256

    @pl.loop(0, window // width)
    def _(step):
        columns = pl.ds(pl.multiple_of(step * width, width), width)
        spectrum_ref[:, columns] = jnp.dot(
            panels_ref[...], forward_ref[:, columns], preferred_element_type=jnp.float32
        ).astype(jnp.bfloat16)

    code = (meta_ref[0:1, :] // block_len) * capacity + meta_ref[1:2, :]
    slots = chosen_ref.shape[0]
    picked = (lax.broadcasted_iota(jnp.int32, (slots, shots), 0) == code).astype(jnp.float32)
    chosen_ref[...] = jnp.dot(
        picked.astype(jnp.bfloat16), turn_ref[...], preferred_element_type=jnp.float32
    ).astype(jnp.bfloat16)
    owners = slots // capacity
    half = jnp.float32(0.5)

    @pl.loop(0, pair * (freqs // width))
    def _(step):
        rec = step // (freqs // width)
        part = lax.rem(step, freqs // width)
        low = pl.ds(pl.multiple_of(part * width, width), width)
        high = pl.ds(pl.multiple_of(freqs + part * width, width), width)
        rows = pl.ds(pl.multiple_of(rec * shots, shots), shots)
        a, b = spectrum_ref[rows, low], spectrum_ref[rows, high]
        keep = keep_ref[:, low].astype(jnp.float32)
        turn = turn_ref[...]
        p = jnp.dot(turn, jnp.concatenate([a, b], axis=0), preferred_element_type=jnp.float32)
        q = jnp.dot(turn, jnp.concatenate([b, -a], axis=0), preferred_element_type=jnp.float32)
        p, q = (p * keep).astype(jnp.bfloat16), (q * keep).astype(jnp.bfloat16)
        chosen = chosen_ref[...]
        ma = jnp.dot(chosen, jnp.concatenate([p, -q], axis=0), preferred_element_type=jnp.float32)
        mb = jnp.dot(chosen, jnp.concatenate([q, p], axis=0), preferred_element_type=jnp.float32)
        first = lax.broadcasted_iota(jnp.int32, (slots, width), 1) + part * width == 0
        ma = jnp.where(first, ma * half, ma).astype(jnp.bfloat16)
        mb = jnp.where(first, mb * half, mb).astype(jnp.bfloat16)
        for owner in range(owners):
            mine = slice(owner * capacity, (owner + 1) * capacity)
            there = pl.ds(pl.multiple_of(rec * capacity, capacity), capacity)
            mixed_ref[owner, there, low] = ma[mine]
            mixed_ref[owner, there, high] = mb[mine]


def filter_records(meta, records, keep_flags, forward, turn, tm_count, block_len):
    shots, freqs = keep_flags.shape
    window = 2 * freqs
    capacity = 2 * shots // tm_count
    vmem = pl.BlockSpec(memory_space=pltpu.VMEM)
    return pl.pallas_call(
        functools.partial(filter_kernel, block_len, capacity),
        out_shape=jax.ShapeDtypeStruct((tm_count, 2 * capacity, window), jnp.bfloat16),
        in_specs=[
            pl.BlockSpec(memory_space=pltpu.SMEM), vmem, vmem, vmem, vmem, vmem,
        ],
        out_specs=vmem,
        scratch_shapes=[
            pltpu.VMEM((records.shape[0] + 4 * window // LANES, LANES), jnp.float32),
            pltpu.VMEM((2 * shots * window // LANES, LANES), jnp.float32),
            pltpu.VMEM((2 * shots, window), jnp.bfloat16),
            pltpu.VMEM((2 * shots, window), jnp.bfloat16),
            pltpu.VMEM((tm_count * capacity, 2 * shots), jnp.bfloat16),
        ],
        compiler_params=pltpu.CompilerParams(vmem_limit_bytes=24 << 20),
        name="filter_records",
    )(meta, meta, records, keep_flags, forward, turn)


def deliver_kernel(
    tm_count, side, batch,
    mixed_ref, forward_ref,
    traces_ref,
    arrived_ref, own_sem, send_sem, recv_sem,
):
    me = lax.axis_index("tm")
    offsets = [(0, 0)] + torus_offsets(side)
    rows = mixed_ref.shape[1]
    capacity = rows // 2
    window = mixed_ref.shape[2]
    barrier = pltpu.get_barrier_semaphore()
    for offset in offsets[1:]:
        pl.semaphore_signal(
            barrier, inc=1, device_id={"tm": tm_peer(me, side, offset, -1)}, device_id_type=MESH
        )
    own = pltpu.make_async_copy(mixed_ref.at[me], arrived_ref.at[0], own_sem)
    own.start()
    pl.semaphore_wait(barrier, tm_count - 1)
    copies = [own]
    for i, offset in enumerate(offsets):
        if i == 0:
            continue
        peer = tm_peer(me, side, offset)
        copies.append(
            pltpu.make_async_remote_copy(
                mixed_ref.at[peer], arrived_ref.at[i], send_sem.at[i], recv_sem.at[i],
                device_id={"tm": peer}, device_id_type=MESH,
            )
        )
        copies[-1].start()
    width = 256
    scale = jnp.float32(4.0 / (window * tm_count * capacity))
    for first in range(0, tm_count, batch):
        for i in range(first, first + batch):
            if i == 0:
                own.wait()
            else:
                copies[i].wait_recv()
        sources = [tm_peer(me, side, offsets[i], -1) for i in range(first, first + batch)]

        @pl.loop(0, window // width)
        def _(step):
            columns = pl.ds(pl.multiple_of(step * width, width), width)
            block = arrived_ref[first : first + batch].reshape(batch * rows, window)
            out = lax.dot_general(
                block, forward_ref[columns, :], NT, preferred_element_type=jnp.float32
            ) * scale
            for i in range(batch):
                for rec in range(2):
                    at = i * rows + rec * capacity
                    for tile in range(width // LANES):
                        traces_ref[
                            step * (width // LANES) + tile,
                            pl.ds(sources[i] * 2 + rec, capacity, stride=2 * tm_count),
                            :,
                        ] = out[at : at + capacity, tile * LANES : (tile + 1) * LANES]

    for copy in copies[1:]:
        copy.wait_send()


def deliver(mixed, forward, batch=4):
    tm_count, rows, window = mixed.shape
    side = int(round(tm_count**0.5))
    dma = pltpu.SemaphoreType.DMA
    return pl.pallas_call(
        functools.partial(deliver_kernel, tm_count, side, batch),
        out_shape=jax.ShapeDtypeStruct((window // LANES, tm_count * rows, LANES), jnp.float32),
        in_specs=[
            pl.BlockSpec(memory_space=pltpu.VMEM),
            pl.BlockSpec(memory_space=pltpu.VMEM),
        ],
        out_specs=pl.BlockSpec(memory_space=pltpu.VMEM),
        scratch_shapes=[
            pltpu.VMEM(mixed.shape, jnp.bfloat16),
            dma, dma((tm_count,)), dma((tm_count,)),
        ],
        compiler_params=pltpu.CompilerParams(
            collective_id=1, has_side_effects=True, vmem_limit_bytes=24 << 20
        ),
        name="deliver_windows",
    )(mixed, forward)


def place_kernel(traces_ref, placed_ref, staged_ref, sem):
    slots, receivers, _ = staged_ref.shape

    def out_copy(slot):
        return pltpu.make_async_copy(staged_ref.at[slot], placed_ref.at[slot], sem.at[slot])

    @pl.loop(0, slots)
    def _(slot):
        for tile in range(traces_ref.shape[0]):
            rows = traces_ref[tile, pl.ds(pl.multiple_of(slot * receivers, receivers), receivers), :]
            staged_ref[slot, :, tile * LANES : (tile + 1) * LANES] = rows.astype(jnp.bfloat16)
        out_copy(slot).start()

    @pl.loop(0, slots)
    def _(slot):
        out_copy(slot).wait()


def place(traces, slots, receivers):
    window = traces.shape[0] * LANES
    return pl.pallas_call(
        place_kernel,
        out_shape=jax.ShapeDtypeStruct((slots, receivers, window), jnp.bfloat16),
        in_specs=[pl.BlockSpec(memory_space=pltpu.VMEM)],
        out_specs=pl.BlockSpec(memory_space=pl.ANY),
        scratch_shapes=[
            pltpu.VMEM((slots, receivers, window), jnp.bfloat16),
            pltpu.SemaphoreType.DMA((slots,)),
        ],
        compiler_params=pltpu.CompilerParams(vmem_limit_bytes=12 << 20),
        name="place_windows",
    )(traces)


def on_device(station_traces, shot_onset_ticks, span_place_index, spectral_keep_flags):
    tm_count, line_count = lax.axis_size("tm"), lax.axis_size("line")
    rec_rows, block_len = station_traces.shape
    shots, freqs = spectral_keep_flags.shape
    window = 2 * freqs
    forward, turn = make_tables(window, shots)
    forward, turn = jnp.asarray(forward), jnp.asarray(turn)
    blocks = station_traces.reshape(tm_count, rec_rows // tm_count, block_len // LANES, LANES)
    blocks = jnp.swapaxes(blocks, 1, 2).reshape(tm_count, -1, LANES)
    tables = (forward, turn, spectral_keep_flags)
    records, meta, forward, turn, keep = exchange(
        blocks, shot_onset_ticks, span_place_index, tables, tm_count, line_count
    )
    mixed = filter_records(
        meta, records, keep, forward, turn, tm_count, block_len
    )
    traces = deliver(mixed, forward)
    return place(traces, 2 * shots // tm_count, rec_rows)


def solution(mesh):
    in_specs = (P("line", "tm"), P("line"), P("line"), P())
    out_specs = P("tm", "line", None)
    return jax.shard_map(
        on_device, mesh=mesh, in_specs=in_specs, out_specs=out_specs, check_vma=False
    )
```
